512 devices in a mesh: dp: 8 (over y_hi, core), seq: 64 (over y_lo, x, z).
Axes of the slice: x: 4, y: 8 (y_hi: 4, y_lo: 2; y = y_hi * 2 + y_lo), z: 8, core: 2. Of those that a mesh axis runs over, the one named last changes fastest.
Arguments:
- queries: bfloat16 [8, 8192, 512], P('dp', 'seq'), may hold values from -6 to 6
- keys: bfloat16 [8, 8192, 512], P('dp', 'seq'), may hold values from -6 to 6
- values: bfloat16 [8, 8192, 512], P('dp', 'seq'), may hold values from -12 to 12
- residual: bfloat16 [8, 8192, 1024], P('dp', 'seq'), may hold values from -3 to 3
- out_proj: bfloat16 [512, 1024], replicated, may hold values from -0.25 to 0.25
- conv_in: bfloat16 [1024, 2048], P(None, 'seq'), may hold values from -0.1875 to 0.1875
- conv_out: bfloat16 [1024, 1024], replicated, may hold values from -0.1875 to 0.1875
- depth_kernel: bfloat16 [31, 1024], replicated, may hold values from -1 to 1
- norm_gain: float32 [1024], replicated, may hold values from 0.25 to 1.75
- cotangent: bfloat16 [8, 8192, 1024], P('dp', 'seq'), may hold values from -6 to 6
Outputs:
- layer_out: bfloat16 [8, 8192, 1024], P('dp', 'seq')
- grad_mid: bfloat16 [8, 8192, 1024], P('dp', 'seq')
- grad_out_proj: float32 [512, 1024], P('seq')
- grad_kernel: float32 [31, 1024], replicated
The draws below stay inside these ranges and needn't reach their ends.
All inputs are finite; a program needn't handle non-finite values.
Results may differ from the reference program's by a relative error of at most 0.015.
Values may be sent and summed in bfloat16 or wider, within the bound.
No kernel may reach another device: no remote copies, remote signals or barrier semaphores. Data moves between devices by JAX's collectives and lax.ppermute only.
A program may use at most 128 MiB of HBM per device.

```python
import math
import jax
import jax.numpy as jnp
from jax import lax

D = 1024
HEADS = 8
DH = 64
KW = 31
BATCH = 8
LENGTH = 8192


def paired_draw(key):
    base = jax.random.fold_in(key, 7)
    first, second = jax.random.split(base, 2)
    shape = (BATCH, LENGTH, HEADS * DH)
    query_draw = jnp.clip(1.5 * jax.random.normal(first, shape, jnp.float32), -6.0, 6.0)
    key_draw = jnp.clip(1.5 * jax.random.normal(second, shape, jnp.float32), -6.0, 6.0)
    return (query_draw, key_draw)


def draw_queries(key, part):
    return paired_draw(key)[0].astype(jnp.bfloat16)


def draw_keys(key, part):
    return paired_draw(key)[1].astype(jnp.bfloat16)


def block_levels(stream_key, dims, shards, least, high):
    gain = 1.0
    for position, shards_of in shards:
        steps = jax.random.uniform(jax.random.fold_in(jax.random.fold_in(stream_key, 6), position), (shards_of,), jnp.float32, least / len(shards), high / len(shards))
        gain = gain * jnp.repeat(jnp.exp(steps), dims[position] // shards_of).reshape((-1,) + (1,) * (len(dims) - 1 - position))
    return gain


def centred(stream_key, dims, spread, most, shards=(), held_as=jnp.bfloat16):
    values = jax.random.normal(stream_key, dims, jnp.float32) * spread
    if len(shards) > 0:
        values = block_levels(stream_key, dims, shards, -0.22, 0.18) * values
    return jnp.clip(values, min=-most, max=most).astype(held_as)


def setup_inputs(seed: int = 0) -> dict:
    key_list = jax.random.split(jax.random.key(seed), 11)
    queries = draw_queries(jax.random.fold_in(key_list[10], 71), 0)
    keys = draw_keys(jax.random.fold_in(key_list[10], 71), 0)
    values = centred(key_list[2], (BATCH, LENGTH, HEADS * DH), 2.0, 12.0, ((0, 8), (1, 64)))
    residual = centred(key_list[3], (BATCH, LENGTH, D), 0.5, 3.0, ((0, 8), (1, 64)))
    out_proj = centred(key_list[4], (HEADS * DH, D), (HEADS * DH) ** -0.5, 0.25)
    conv_in = centred(key_list[5], (D, 2 * D), D ** -0.5, 0.1875, ((1, 64),))
    conv_out = centred(key_list[6], (D, D), D ** -0.5, 0.1875)
    depth_kernel = centred(key_list[7], (KW, D), KW ** -0.5, 1.0)
    norm_gain = jnp.clip(1.0 + 0.15 * jax.random.normal(key_list[8], (D,), jnp.float32), 0.25, 1.75)
    cotangent = centred(key_list[9], (BATCH, LENGTH, D), 1.0, 6.0, ((0, 8), (1, 64)))
    return dict(queries=queries, keys=keys, values=values, residual=residual, out_proj=out_proj, conv_in=conv_in, conv_out=conv_out, depth_kernel=depth_kernel, norm_gain=norm_gain, cotangent=cotangent)


norm_epsilon = 1e-05

def attend_one(triple):
    query, key_rows, value_rows = triple
    length = query.shape[0]
    block = math.gcd(length, 512)
    query_blocks = query.reshape(length // block, block, query.shape[1])

    def one_block(query_block):
        scores = lax.dot_general(query_block, key_rows, (((1,), (1,)), ((), ())), preferred_element_type=jnp.float32) * DH ** (-0.5)
        highest = lax.optimization_barrier(jnp.max(scores, axis=1, keepdims=True))
        expo = jnp.exp(scores - highest)
        total = lax.optimization_barrier(jnp.sum(expo, axis=1, keepdims=True))
        weights = expo.astype(jnp.bfloat16)
        mixed = jnp.dot(weights, value_rows, preferred_element_type=jnp.float32)
        return (mixed / total).astype(jnp.bfloat16)
    return lax.map(one_block, query_blocks).reshape(length, query.shape[1])

def layer_norm(mid):
    wide = mid.astype(jnp.float32)
    centered = wide - lax.optimization_barrier(jnp.mean(wide, axis=-1, keepdims=True))
    rscale = lax.rsqrt(lax.optimization_barrier(jnp.mean(centered * centered, axis=-1, keepdims=True)) + norm_epsilon)
    return (centered * rscale, rscale)

def depth_forward(padded, kernel, rows):
    total = jnp.zeros((padded.shape[0], rows, padded.shape[2]), jnp.float32)
    for offset in range(KW):
        total = total + kernel[offset].astype(jnp.float32) * padded[:, offset:offset + rows].astype(jnp.float32)
    return total

def depth_backward(padded, kernel, rows):
    total = jnp.zeros((padded.shape[0], rows, padded.shape[2]), jnp.float32)
    reach = (KW - 1) // 2
    for offset in range(KW):
        begin = 2 * reach - offset
        total = total + kernel[offset].astype(jnp.float32) * padded[:, begin:begin + rows].astype(jnp.float32)
    return total

def kernel_terms(padded, grad_conv, rows):
    terms = []
    for offset in range(KW):
        product = padded[:, offset:offset + rows].astype(jnp.float32) * grad_conv.astype(jnp.float32)
        terms.append(lax.optimization_barrier(jnp.sum(product, axis=(0, 1))))
    return jnp.stack(terms, axis=0)

def reference(queries, keys, values, residual, out_proj, conv_in, conv_out, depth_kernel, norm_gain, cotangent):
    batch, length, width = queries.shape
    model = residual.shape[2]
    reach = (KW - 1) // 2

    def split_heads(array):
        return array.reshape(batch, length, HEADS, DH).transpose(0, 2, 1, 3).reshape(batch * HEADS, length, DH)
    heads_out = lax.map(attend_one, (split_heads(queries), split_heads(keys), split_heads(values)))
    attended = heads_out.reshape(batch, HEADS, length, DH).transpose(0, 2, 1, 3).reshape(batch * length, width)
    flat_resid = residual.reshape(batch * length, model).astype(jnp.float32)
    mid = (flat_resid + jnp.dot(attended, out_proj, preferred_element_type=jnp.float32)).astype(jnp.bfloat16)
    hat, rscale = layer_norm(mid)
    normed = (hat * norm_gain).astype(jnp.bfloat16)
    proj = jnp.dot(normed, conv_in, preferred_element_type=jnp.float32)
    value_half = proj[:, :model]
    gate_half = jax.nn.sigmoid(proj[:, model:])
    gated = (value_half * gate_half).astype(jnp.bfloat16).reshape(batch, length, model)
    padded = jnp.pad(gated, ((0, 0), (reach, reach), (0, 0)))
    conv = depth_forward(padded, depth_kernel, length)
    act = (conv * jax.nn.sigmoid(conv)).astype(jnp.bfloat16).reshape(batch * length, model)
    layer_out = (mid.astype(jnp.float32) + jnp.dot(act, conv_out, preferred_element_type=jnp.float32)).astype(jnp.bfloat16)
    flat_cot = cotangent.reshape(batch * length, model)
    grad_act = lax.dot_general(flat_cot, conv_out, (((1,), (1,)), ((), ())), preferred_element_type=jnp.float32)
    sig_conv = jax.nn.sigmoid(conv).reshape(batch * length, model)
    conv_flat = conv.reshape(batch * length, model)
    grad_conv = (grad_act * sig_conv * (1.0 + conv_flat * (1.0 - sig_conv))).astype(jnp.bfloat16).reshape(batch, length, model)
    grad_padded = jnp.pad(grad_conv, ((0, 0), (reach, reach), (0, 0)))
    grad_gated = depth_backward(grad_padded, depth_kernel, length).reshape(batch * length, model)
    grad_kernel = kernel_terms(padded, grad_conv, length)
    grad_proj = jnp.concatenate([grad_gated * gate_half, grad_gated * value_half * gate_half * (1.0 - gate_half)], axis=1).astype(jnp.bfloat16)
    grad_normed = lax.dot_general(grad_proj, conv_in, (((1,), (1,)), ((), ())), preferred_element_type=jnp.float32)
    scaled = grad_normed * norm_gain
    inner = scaled - lax.optimization_barrier(jnp.mean(scaled, axis=1, keepdims=True)) - hat * lax.optimization_barrier(jnp.mean(scaled * hat, axis=1, keepdims=True))
    grad_mid = (flat_cot.astype(jnp.float32) + rscale * inner).astype(jnp.bfloat16)
    grad_out_proj = lax.dot_general(attended, grad_mid, (((0,), (0,)), ((), ())), preferred_element_type=jnp.float32)
    return (layer_out.reshape(batch, length, model), grad_mid.reshape(batch, length, model), grad_out_proj, grad_kernel)
```

```python
import math

import jax
import jax.numpy as jnp
from jax import lax
from jax.experimental import pallas as pl
from jax.experimental.pallas import tpu as pltpu
from jax.sharding import Mesh, PartitionSpec as P

HEADS = 8
DH = 64
KW = 31
REACH = (KW - 1) // 2
norm_epsilon = 1e-05

F32 = jnp.float32
BF16 = jnp.bfloat16

YX = ("yl", "x")
SEQ = ("yl", "x", "z")
NT = (((1,), (1,)), ((), ()))


def pack_kernel(q_ref, k_ref, v_ref, o_ref):
    for pair in range(HEADS // 2):
        cols = pl.ds(pair * 128, 128)
        q_t = q_ref[:, cols].astype(F32).T.astype(BF16)
        v_t = v_ref[:, cols].astype(F32).T.astype(BF16)
        upper = k_ref[0:64, cols].astype(F32)
        lower = k_ref[64:128, cols].astype(F32)
        lane = lax.broadcasted_iota(jnp.int32, upper.shape, 1)
        first = jnp.where(lane < 64, upper, pltpu.roll(lower, 64, 1)).astype(BF16)
        second = jnp.where(lane < 64, pltpu.roll(upper, 64, 1), lower).astype(BF16)
        for half, packed in ((0, first), (1, second)):
            head = 2 * pair + half
            o_ref[head, 0] = q_t[half * 64 : half * 64 + 64]
            o_ref[head, 1] = packed
            o_ref[head, 2] = v_t[half * 64 : half * 64 + 64]


def pack(q, k, v):
    return pl.pallas_call(
        pack_kernel,
        out_shape=jax.ShapeDtypeStruct((HEADS, 3, 64, 128), BF16),
    )(q, k, v)


SCALE = DH ** (-0.5) * math.log2(math.e)
QB = 256


def attend_kernel(q_ref, kv_ref, o_ref, r_lo, r_hi, top, acc):
    step = pl.program_id(0)
    count = q_ref.shape[0]
    width = count * 128

    @pl.when(step == 0)
    def _():
        for i in range(count):
            scaled = q_ref[i].astype(F32) * SCALE
            high = scaled.astype(BF16)
            low = (scaled - high.astype(F32)).astype(BF16)
            none = jnp.zeros_like(high)
            cols = pl.ds(i * 128, 128)
            r_lo[:, cols] = jnp.concatenate([high, none, low, none], axis=0)
            r_hi[:, cols] = jnp.concatenate([none, high, none, low], axis=0)
        top[...] = jnp.full(top.shape, -jnp.inf, F32)
        acc[...] = jnp.zeros(acc.shape, F32)

    sources = kv_ref.shape[0]
    packed = kv_ref[:, 0].reshape(sources * 64, 128)
    keys = jnp.concatenate([packed, packed], axis=1)
    values = jnp.concatenate([kv_ref[s, 1] for s in range(sources)], axis=1)
    values = jnp.concatenate([values, jnp.ones((16, sources * 128), BF16)], axis=0)
    for block in range(width // QB):
        cols = pl.ds(block * QB, QB)
        s_lo = jnp.dot(keys, r_lo[:, cols], preferred_element_type=F32)
        s_hi = jnp.dot(keys, r_hi[:, cols], preferred_element_type=F32)
        before = top[:, cols]
        highest = jnp.maximum(
            before, jnp.max(jnp.maximum(s_lo, s_hi), axis=0, keepdims=True)
        )
        top[:, cols] = highest
        p_lo = jnp.exp2(s_lo - highest).astype(BF16)
        p_hi = jnp.exp2(s_hi - highest).astype(BF16)
        pieces = []
        for s in range(sources):
            pieces.append(p_lo[s * 64 : s * 64 + 64])
            pieces.append(p_hi[s * 64 : s * 64 + 64])
        weights = jnp.concatenate(pieces, axis=0)
        mixed = jnp.dot(values, weights, preferred_element_type=F32)
        acc[:, cols] = acc[:, cols] * jnp.exp2(before - highest) + mixed

    @pl.when(step == pl.num_programs(0) - 1)
    def _():
        done = (acc[0:64] / acc[64:65]).astype(BF16)
        for i in range(count):
            o_ref[i] = done[:, i * 128 : i * 128 + 128]


def attend(q_t, kv):
    count = q_t.shape[0]
    sources = kv.shape[0]
    chunk = 8
    return pl.pallas_call(
        attend_kernel,
        grid=(sources // chunk,),
        in_specs=[
            pl.BlockSpec((count, 64, 128), lambda i: (0, 0, 0)),
            pl.BlockSpec((chunk, 2, 64, 128), lambda i: (i, 0, 0, 0)),
        ],
        out_specs=pl.BlockSpec((count, 64, 128), lambda i: (0, 0, 0)),
        out_shape=jax.ShapeDtypeStruct((count, 64, 128), BF16),
        scratch_shapes=[
            pltpu.VMEM((256, count * 128), BF16),
            pltpu.VMEM((256, count * 128), BF16),
            pltpu.VMEM((1, count * 128), F32),
            pltpu.VMEM((80, count * 128), F32),
        ],
        compiler_params=pltpu.CompilerParams(vmem_limit_bytes=56 * 1024 * 1024),
    )(q_t, kv)


def swap(array, axes):
    return lax.all_to_all(array, axes, split_axis=0, concat_axis=0, tiled=True)


def spread(array, axes, count):
    return swap(jnp.broadcast_to(array[None], (count,) + array.shape), axes)


def neighbours(rows, width):
    count = 64
    head = rows[:width]
    tail = rows[rows.shape[0] - width :]
    before = lax.ppermute(tail, SEQ, [(i, i + 1) for i in range(count - 1)])
    after = lax.ppermute(head, SEQ, [(i + 1, i) for i in range(count - 1)])
    return jnp.concatenate([before, rows, after], axis=0)


def layer_norm(mid):
    wide = mid.astype(F32)
    centered = wide - jnp.mean(wide, axis=-1, keepdims=True)
    rscale = lax.rsqrt(jnp.mean(centered * centered, axis=-1, keepdims=True) + norm_epsilon)
    return centered * rscale, rscale


def depth_forward(padded, kernel, rows):
    total = jnp.zeros((rows, padded.shape[1]), F32)
    for offset in range(KW):
        total = total + kernel[offset].astype(F32) * padded[offset : offset + rows].astype(F32)
    return total


def depth_backward(padded, kernel, rows):
    total = jnp.zeros((rows, padded.shape[1]), F32)
    for offset in range(KW):
        begin = 2 * REACH - offset
        total = total + kernel[offset].astype(F32) * padded[begin : begin + rows].astype(F32)
    return total


def kernel_terms(padded, grad_conv, rows):
    wide = grad_conv.astype(F32)
    terms = []
    for offset in range(KW):
        terms.append(jnp.sum(padded[offset : offset + rows].astype(F32) * wide, axis=0))
    terms.append(jnp.zeros_like(terms[0]))
    return jnp.stack(terms, axis=0)


def body(
    queries, keys, values, residual, out_proj, conv_in, conv_out, depth_kernel, norm_gain, cotangent
):
    rows = queries.shape[1]
    model = residual.shape[2]
    core = lax.axis_index("core")

    turned = conv_in.T
    share = lax.dynamic_slice_in_dim(turned, core * (model // 2), model // 2, axis=1)
    share = lax.all_gather(share, YX, axis=0, tiled=False)
    share = lax.all_gather(share, "z", axis=0, tiled=False)
    both = lax.all_gather(share, "core", axis=0, tiled=False)
    halves = [
        both[c].transpose(1, 0, 2, 3).reshape(2 * model, model // 2) for c in range(2)
    ]

    cot = cotangent[0]
    cot_wide = neighbours(cot, REACH)
    grad_act = lax.dot_general(cot_wide, conv_out, NT, preferred_element_type=F32)

    sent = pack(queries[0], keys[0], values[0])
    got = swap(sent, "z")
    kv = spread(got[:, 1:], YX, 8).reshape(64, 2, 64, 128)
    attended_t = swap(attend(got[:, 0], kv), "z").reshape(HEADS * DH, rows)

    flat_resid = residual[0].astype(F32)
    mid = (
        flat_resid
        + lax.dot_general(
            attended_t, out_proj, (((0,), (0,)), ((), ())), preferred_element_type=F32
        )
    ).astype(BF16)
    hat, rscale = layer_norm(mid)
    normed = (hat * norm_gain).astype(BF16)
    proj = lax.dot_general(
        normed[:, : model // 2], halves[0], NT, preferred_element_type=F32
    ) + lax.dot_general(normed[:, model // 2 :], halves[1], NT, preferred_element_type=F32)
    value_half = proj[:, :model]
    gate_half = jax.nn.sigmoid(proj[:, model:])
    gated = (value_half * gate_half).astype(BF16)
    padded = neighbours(gated, 2 * REACH)
    conv = depth_forward(padded, depth_kernel, rows + 2 * REACH)
    sig_conv = jax.nn.sigmoid(conv)
    act = (conv * sig_conv)[REACH : REACH + rows].astype(BF16)
    layer_out = (mid.astype(F32) + jnp.dot(act, conv_out, preferred_element_type=F32)).astype(BF16)
    grad_padded = (grad_act * sig_conv * (1.0 + conv * (1.0 - sig_conv))).astype(BF16)
    grad_gated = depth_backward(grad_padded, depth_kernel, rows)
    grad_kernel = kernel_terms(
        padded[REACH : REACH + rows + 2 * REACH], grad_padded[REACH : REACH + rows], rows
    )
    grad_proj = jnp.concatenate(
        [grad_gated * gate_half, grad_gated * value_half * gate_half * (1.0 - gate_half)], axis=1
    ).astype(BF16)
    grad_normed = jnp.concatenate(
        [jnp.dot(grad_proj, half, preferred_element_type=F32) for half in halves], axis=1
    )
    scaled = grad_normed * norm_gain
    inner = (
        scaled
        - jnp.mean(scaled, axis=1, keepdims=True)
        - hat * jnp.mean(scaled * hat, axis=1, keepdims=True)
    )
    grad_mid = (cot.astype(F32) + rscale * inner).astype(BF16)
    partial = jnp.dot(attended_t, grad_mid, preferred_element_type=F32)

    by_core = partial.reshape(8, 8, 2, 4, model).transpose(2, 0, 1, 3, 4).reshape(2, 256, model)
    both_sums = jnp.concatenate([by_core, grad_kernel.reshape(2, 16, model)], axis=1)
    sums = jnp.sum(swap(both_sums.astype(BF16), "core").astype(F32), axis=0)

    def joined(first, second, count):
        second = jnp.broadcast_to(second[None], (count,) + second.shape)
        return jnp.concatenate([first, second], axis=1)

    sums = joined(sums[:256].reshape(8, 32, model), sums[256:], 8)
    sums = jnp.sum(swap(sums.astype(BF16), YX).astype(F32), axis=0)
    sums = joined(sums[:32].reshape(8, 4, model), sums[32:], 8)
    sums = jnp.sum(swap(sums.astype(BF16), "z").astype(F32), axis=0)
    sums = jnp.sum(spread(sums, "yh", 4), axis=0)
    sums = spread(sums, "core", 2)
    grad_out_proj = sums[:, :4].reshape(8, model)
    grad_kernel = sums[:, 4:].reshape(32, model)[:KW]
    return layer_out[None], grad_mid[None], grad_out_proj, grad_kernel


def solution(mesh):
    split = Mesh(mesh.devices.reshape(4, 2, 2, 4, 8), ("yh", "core", "yl", "x", "z"))
    rows = P(("yh", "core"), SEQ, None)
    return jax.shard_map(
        body,
        mesh=split,
        in_specs=(rows, rows, rows, rows, P(), P(None, SEQ), P(), P(), P(), rows),
        out_specs=(rows, rows, P(SEQ, None), P()),
        check_vma=False,
    )
```

```python
import math

import jax
import jax.numpy as jnp
from jax import lax
from jax.experimental import pallas as pl
from jax.experimental.pallas import tpu as pltpu
from jax.sharding import Mesh, PartitionSpec as P


HEADS = 8
DH = 64
KW = 31
norm_epsilon = 1e-05

F32 = jnp.float32
BF16 = jnp.bfloat16

YX = ("yl", "x")
SEQ = ("yl", "x", "z")
NT = (((1,), (1,)), ((), ()))


def pack_kernel(q_ref, k_ref, v_ref, w_ref, o_ref):
    for pair in range(HEADS // 2):
        cols = pl.ds(pair * 128, 128)
        q_t = q_ref[:, cols].astype(F32).T.astype(BF16)
        v_t = v_ref[:, cols].astype(F32).T.astype(BF16)
        upper = k_ref[0:64, cols].astype(F32)
        lower = k_ref[64:128, cols].astype(F32)
        lane = lax.broadcasted_iota(jnp.int32, upper.shape, 1)
        first = jnp.where(lane < 64, upper, pltpu.roll(lower, 64, 1)).astype(BF16)
        second = jnp.where(lane < 64, pltpu.roll(upper, 64, 1), lower).astype(BF16)
        for half, packed in ((0, first), (1, second)):
            head = 2 * pair + half
            o_ref[head, 0] = q_t[half * 64 : half * 64 + 64]
            o_ref[head, 1] = packed
            o_ref[head, 2] = v_t[half * 64 : half * 64 + 64]
    for half in range(2):
        turned = jnp.concatenate(
            [
                w_ref[half * 256 + b * 128 : half * 256 + b * 128 + 128, :].astype(F32).T
                for b in range(2)
            ],
            axis=0,
        ).astype(BF16)
        for head in range(HEADS):
            o_ref[head, 3 + half] = turned


def pack(q, k, v, w):
    return pl.pallas_call(
        pack_kernel,
        out_shape=jax.ShapeDtypeStruct((HEADS, 5, 64, 128), BF16),
    )(q, k, v, w)


SCALE = DH ** (-0.5) * math.log2(math.e)
QB = 256
SMALLEST = 2.0**-90
COST = pl.CostEstimate(flops=2**34, transcendentals=2**23, bytes_accessed=2**21)


def block_of(kv_ref, start, sources):
    packed = kv_ref[pl.ds(start, sources), 0].reshape(sources * 64, 128)
    keys = jnp.concatenate([packed, packed], axis=1)
    values = jnp.concatenate([kv_ref[start + s, 1] for s in range(sources)], axis=1)
    return keys, jnp.concatenate([values, jnp.ones((16, sources * 128), BF16)], axis=0)


def interleave(p_lo, p_hi, sources):
    pieces = []
    for s in range(sources):
        pieces.append(p_lo[s * 64 : s * 64 + 64])
        pieces.append(p_hi[s * 64 : s * 64 + 64])
    return jnp.concatenate(pieces, axis=0)


def attend_kernel(q_ref, kv_ref, o_ref, r_lo, r_hi, top, acc):
    count = q_ref.shape[0]
    sources = kv_ref.shape[0]
    blocks = count * 128 // QB
    group = 16
    whole = sources

    lane = lax.broadcasted_iota(jnp.int32, (128, 128), 1) < 64
    row = lax.broadcasted_iota(jnp.int32, (128, 128), 0) < 64
    same = (lane == row).astype(BF16)

    def longest(i, so_far):
        wide = kv_ref[pl.ds(i * group, group), 0].reshape(group * 64, 128).astype(F32)
        squares = (wide * wide).astype(BF16)
        return jnp.maximum(
            so_far,
            jnp.max(jnp.dot(squares, same, preferred_element_type=F32), axis=0, keepdims=True),
        )

    key_square = jnp.max(
        lax.fori_loop(0, sources // group, longest, jnp.zeros((1, 128), F32)),
        axis=1,
        keepdims=True,
    ) * 1.02

    for i in range(count):
        scaled = q_ref[i].astype(F32) * SCALE
        high = scaled.astype(BF16)
        low = (scaled - high.astype(F32)).astype(BF16)
        none = jnp.zeros_like(high)
        cols = pl.ds(i * 128, 128)
        r_lo[:, cols] = jnp.concatenate([high, none, low, none], axis=0)
        r_hi[:, cols] = jnp.concatenate([none, high, none, low], axis=0)
        top[:, cols] = jnp.sqrt(jnp.sum(scaled * scaled, axis=0, keepdims=True) * key_square)
    acc[...] = jnp.zeros(acc.shape, F32)

    def direct(i, carry):
        keys, values = block_of(kv_ref, i * whole, whole)
        for block in range(blocks):
            cols = pl.ds(block * QB, QB)
            bound = top[:, cols]
            s_lo = jnp.dot(keys, r_lo[:, cols], preferred_element_type=F32)
            p_lo = jnp.exp2(s_lo - bound).astype(BF16)
            s_hi = jnp.dot(keys, r_hi[:, cols], preferred_element_type=F32)
            p_hi = jnp.exp2(s_hi - bound).astype(BF16)
            acc[:, cols] += jnp.dot(
                values, interleave(p_lo, p_hi, whole), preferred_element_type=F32
            )
        return carry

    lax.fori_loop(0, sources // whole, direct, 0)

    @pl.when(jnp.min(acc[64:65]) < SMALLEST)
    def _():
        top[...] = jnp.full(top.shape, -jnp.inf, F32)
        acc[...] = jnp.zeros(acc.shape, F32)

        def online(i, carry):
            keys, values = block_of(kv_ref, i, 1)
            for block in range(blocks):
                cols = pl.ds(block * QB, QB)
                s_lo = jnp.dot(keys, r_lo[:, cols], preferred_element_type=F32)
                s_hi = jnp.dot(keys, r_hi[:, cols], preferred_element_type=F32)
                before = top[:, cols]
                highest = jnp.maximum(
                    before, jnp.max(jnp.maximum(s_lo, s_hi), axis=0, keepdims=True)
                )
                top[:, cols] = highest
                p_lo = jnp.exp2(s_lo - highest).astype(BF16)
                p_hi = jnp.exp2(s_hi - highest).astype(BF16)
                mixed = jnp.dot(values, interleave(p_lo, p_hi, 1), preferred_element_type=F32)
                acc[:, cols] = acc[:, cols] * jnp.exp2(before - highest) + mixed
            return carry

        lax.fori_loop(0, sources, online, 0)

    done = (acc[0:64] / acc[64:65]).astype(BF16)
    for i in range(count):
        o_ref[i] = done[:, i * 128 : i * 128 + 128]


def attend(q_t, kv):
    count = q_t.shape[0]
    return pl.pallas_call(
        attend_kernel,
        out_shape=jax.ShapeDtypeStruct((count, 64, 128), BF16),
        scratch_shapes=[
            pltpu.VMEM((256, count * 128), BF16),
            pltpu.VMEM((256, count * 128), BF16),
            pltpu.VMEM((1, count * 128), F32),
            pltpu.VMEM((80, count * 128), F32),
        ],
        cost_estimate=COST,
        compiler_params=pltpu.CompilerParams(vmem_limit_bytes=56 * 1024 * 1024),
    )(q_t, kv)


STEPS = 4


def columns_of(w_ref, half):
    count = w_ref.shape[1] * 32
    return jnp.concatenate(
        [w_ref[half, :, b].reshape(count, 128) for b in range(4)], axis=1
    )


def gate_kernel(
    core_ref, att_ref, out_proj_ref, residual_ref, gain_ref, cot_ref, own_ref, other_ref,
    mid_ref, hat_ref, rscale_ref, value_ref, gate_ref, gated_ref, first_ref, last_ref, normed,
):
    step = pl.program_id(0)
    core = core_ref[0]
    half = normed.shape[2]

    @pl.when(step == 0)
    def _():
        att = att_ref[...].astype(F32).T.astype(BF16)
        mid = (
            residual_ref[...].astype(F32)
            + jnp.dot(att, out_proj_ref[...], preferred_element_type=F32)
        ).astype(BF16)
        mid_ref[...] = mid
        wide = mid.astype(F32)
        centered = wide - jnp.mean(wide, axis=1, keepdims=True)
        rscale = lax.rsqrt(jnp.mean(centered * centered, axis=1, keepdims=True) + norm_epsilon)
        hat = centered * rscale
        hat_ref[...] = hat
        rscale_ref[...] = jnp.broadcast_to(rscale, rscale_ref.shape)
        scaled = (hat * gain_ref[...]).astype(BF16)
        normed[0] = scaled[:, :half]
        normed[1] = scaled[:, half:]

    def project(part):
        return lax.dot_general(
            normed[core], columns_of(own_ref, part), NT, preferred_element_type=F32
        ) + lax.dot_general(
            normed[1 - core], columns_of(other_ref, part), NT, preferred_element_type=F32
        )

    value = project(0)
    gate = jax.nn.sigmoid(project(1))
    value_ref[...] = value
    gate_ref[...] = gate
    gated = (value * gate).astype(BF16)
    gated_ref[...] = gated
    rows = gated.shape[0]
    first_ref[0:32] = gated[0:32]
    first_ref[32:48] = cot_ref[0:16]
    last_ref[0:32] = gated[rows - 32 :]
    last_ref[32:48] = cot_ref[rows - 16 :]


def gate(core, att, out_proj, residual, gain, cot, own, other):
    rows, model = residual.shape
    part = model // STEPS
    whole = lambda *shape: pl.BlockSpec(shape, lambda i: (0,) * len(shape))
    block = lambda count: pl.BlockSpec((count, part), lambda i: (0, i))
    weights = pl.BlockSpec((2, part // 32, 4, 32, 128), lambda i: (0, i, 0, 0, 0))
    array = jax.ShapeDtypeStruct
    return pl.pallas_call(
        gate_kernel,
        grid=(STEPS,),
        in_specs=[
            pl.BlockSpec(memory_space=pltpu.SMEM),
            whole(*att.shape),
            whole(*out_proj.shape),
            whole(rows, model),
            whole(1, model),
            block(rows),
            weights,
            weights,
        ],
        out_specs=[
            whole(rows, model),
            whole(rows, model),
            whole(rows, 128),
            block(rows),
            block(rows),
            block(rows),
            block(48),
            block(48),
        ],
        out_shape=[
            array((rows, model), BF16),
            array((rows, model), F32),
            array((rows, 128), F32),
            array((rows, model), F32),
            array((rows, model), F32),
            array((rows, model), BF16),
            array((48, model), BF16),
            array((48, model), BF16),
        ],
        scratch_shapes=[pltpu.VMEM((2, rows, model // 2), BF16)],
        compiler_params=pltpu.CompilerParams(vmem_limit_bytes=56 * 1024 * 1024),
    )(core, att, out_proj, residual, gain, cot, own, other)


def back_kernel(
    core_ref, before_ref, after_ref, gated_ref, cot_before_ref, cot_after_ref, cot_ref,
    conv_out_ref, taps_ref, value_ref, gate_ref, own_ref, other_ref, mid_ref, hat_ref, rscale_ref,
    gain_ref, att_ref,
    layer_ref, grad_mid_ref, sums_ref,
    cot_wide, padded, gradient, layer_sum, normed_grad,
):
    step = pl.program_id(0)
    core = core_ref[0]
    rows = gated_ref.shape[0]
    tiles = padded.shape[0]

    @pl.when(step == 0)
    def _():
        cot_wide[0:16] = cot_before_ref[32:48]
        cot_wide[16 : 16 + rows] = cot_ref[...]
        cot_wide[16 + rows : 32 + rows] = cot_after_ref[32:48]
        layer_sum[...] = jnp.zeros(layer_sum.shape, F32)
        normed_grad[...] = jnp.zeros(normed_grad.shape, F32)

    for t in range(tiles):
        lanes = slice(t * 128, t * 128 + 128)
        padded[t, 0:32] = before_ref[0:32, lanes].astype(F32)
        padded[t, 32 : 32 + rows] = gated_ref[:, lanes].astype(F32)
        padded[t, 32 + rows : 64 + rows] = after_ref[0:32, lanes].astype(F32)

    weights = conv_out_ref[...]
    grad_act = lax.dot_general(cot_wide[...], weights, NT, preferred_element_type=F32)
    acts = []
    chunk = (rows + 32) // 2
    for t in range(tiles):
        lanes = slice(t * 128, t * 128 + 128)
        pieces = []
        for part in range(2):
            begin = part * chunk
            conv = jnp.zeros((chunk, 128), F32)
            for k in range(KW):
                conv = conv + taps_ref[k : k + 1, lanes] * padded[t, pl.ds(begin + k + 1, chunk)]
            sig = jax.nn.sigmoid(conv)
            pieces.append(conv * sig)
            gradient[t, begin : begin + chunk] = (
                (grad_act[begin : begin + chunk, lanes] * sig * (1.0 + conv * (1.0 - sig)))
                .astype(BF16)
                .astype(F32)
            )
        acts.append(jnp.concatenate(pieces, axis=0)[16 : 16 + rows])
    act = jnp.concatenate(acts, axis=1).astype(BF16)
    layer_sum[...] += jnp.dot(act, weights, preferred_element_type=F32)

    gated_grads = []
    for t in range(tiles):
        lanes = slice(t * 128, t * 128 + 128)
        pieces = []
        for part in range(2):
            begin = part * (rows // 2)
            total = jnp.zeros((rows // 2, 128), F32)
            for k in range(KW):
                total = total + taps_ref[k : k + 1, lanes] * gradient[
                    t, pl.ds(begin + 31 - k, rows // 2)
                ]
            pieces.append(total)
        gated_grads.append(jnp.concatenate(pieces, axis=0))

        inner = gradient[t, 16 : 16 + rows]
        terms = []
        for k in range(KW):
            terms.append(
                jnp.sum(padded[t, pl.ds(k + 17, rows)] * inner, axis=0, keepdims=True)
            )
        terms.append(jnp.zeros((1, 128), F32))
        tile = step * tiles + t
        sums_ref[tile // 4, 64:68, tile % 4] = (
            jnp.concatenate(terms, axis=0).astype(BF16).reshape(4, 8, 128)
        )

    grad_gated = jnp.concatenate(gated_grads, axis=1)
    value = value_ref[...]
    gate = gate_ref[...]
    to_value = (grad_gated * gate).astype(BF16)
    to_gate = (grad_gated * value * gate * (1.0 - gate)).astype(BF16)
    for place, ref in ((core, own_ref), (1 - core, other_ref)):
        normed_grad[place] += jnp.dot(
            to_value, columns_of(ref, 0), preferred_element_type=F32
        ) + jnp.dot(to_gate, columns_of(ref, 1), preferred_element_type=F32)

    @pl.when(step == pl.num_programs(0) - 1)
    def _():
        layer_ref[...] = (mid_ref[...].astype(F32) + layer_sum[...]).astype(BF16)
        hat = hat_ref[...]
        scaled = jnp.concatenate([normed_grad[0], normed_grad[1]], axis=1) * gain_ref[...]
        inner = (
            scaled
            - jnp.mean(scaled, axis=1, keepdims=True)
            - hat * jnp.mean(scaled * hat, axis=1, keepdims=True)
        )
        grad_mid = (cot_ref_f32(cot_ref) + rscale_ref[:, 0:1] * inner).astype(BF16)
        grad_mid_ref[...] = grad_mid
        for c in range(2):
            for b in range(4):
                cols = slice(c * 512 + b * 128, c * 512 + b * 128 + 128)
                product = jnp.dot(att_ref[...], grad_mid[:, cols], preferred_element_type=F32)
                sums_ref[c, 0:64, b] = product.astype(BF16).reshape(64, 8, 128)


def cot_ref_f32(ref):
    return ref[...].astype(F32)


def back(core, before, after, gated, cot, conv_out, taps, value, gate_half, own, other, mid, hat,
         rscale, gain, att):
    rows, model = gated.shape
    part = model // STEPS
    whole = lambda *shape: pl.BlockSpec(shape, lambda i: (0,) * len(shape))
    block = lambda count: pl.BlockSpec((count, part), lambda i: (0, i))
    weights = pl.BlockSpec((2, part // 32, 4, 32, 128), lambda i: (0, i, 0, 0, 0))
    array = jax.ShapeDtypeStruct
    return pl.pallas_call(
        back_kernel,
        grid=(STEPS,),
        in_specs=[
            pl.BlockSpec(memory_space=pltpu.SMEM),
            block(48),
            block(48),
            block(rows),
            whole(48, model),
            whole(48, model),
            whole(rows, model),
            pl.BlockSpec((part, model), lambda i: (i, 0)),
            block(KW + 1),
            block(rows),
            block(rows),
            weights,
            weights,
            whole(rows, model),
            whole(rows, model),
            whole(rows, 128),
            whole(1, model),
            whole(*att.shape),
        ],
        out_specs=[
            whole(rows, model),
            whole(rows, model),
            whole(2, 68, 4, 8, 128),
        ],
        out_shape=[
            array((rows, model), BF16),
            array((rows, model), BF16),
            array((2, 68, 4, 8, 128), BF16),
        ],
        scratch_shapes=[
            pltpu.VMEM((rows + 32, model), BF16),
            pltpu.VMEM((part // 128, rows + 64, 128), F32),
            pltpu.VMEM((part // 128, rows + 32, 128), F32),
            pltpu.VMEM((rows, model), F32),
            pltpu.VMEM((2, rows, model // 2), F32),
        ],
        compiler_params=pltpu.CompilerParams(vmem_limit_bytes=56 * 1024 * 1024),
    )(core, before, after, gated, before, after, cot, conv_out, taps, value, gate_half, own, other,
      mid, hat, rscale, gain, att)


def swap(array, axes):
    return lax.all_to_all(array, axes, split_axis=0, concat_axis=0, tiled=True)


def spread(array, axes, count):
    return swap(jnp.broadcast_to(array[None], (count,) + array.shape), axes)


def body(
    queries, keys, values, residual, out_proj, conv_in, conv_out, depth_kernel, norm_gain, cotangent
):
    rows = queries.shape[1]
    model = residual.shape[2]
    core = lax.axis_index("core")
    place = core.astype(jnp.int32).reshape(1)
    gain = norm_gain.reshape(1, model)
    cot = cotangent[0]
    taps = jnp.pad(depth_kernel.astype(F32), ((0, 1), (0, 0)))

    share = lax.dynamic_slice_in_dim(conv_in, core * (model // 2), model // 2, axis=0)
    sent = pack(queries[0], keys[0], values[0], share)
    got = swap(sent, "z")
    kv = spread(got[:, 1:3], YX, 8).reshape(64, 2, 64, 128)
    own = spread(got[:, 3:5], YX, 8).reshape(2, 32, 4, 32, 128)
    attended = attend(got[:, 0], kv)
    other = lax.ppermute(own, "core", [(0, 1), (1, 0)])
    att = swap(attended, "z").reshape(HEADS * DH, rows)

    mid, hat, rscale, value_half, gate_half, gated, first, last = gate(
        place, att, out_proj, residual[0], gain, cot, own, other
    )
    count = 64
    before = lax.ppermute(last, SEQ, [(i, i + 1) for i in range(count - 1)])
    after = lax.ppermute(first, SEQ, [(i + 1, i) for i in range(count - 1)])
    layer_out, grad_mid, sums = back(
        place, before, after, gated, cot, conv_out, taps, value_half, gate_half, own, other, mid,
        hat, rscale, gain, att,
    )

    sums = jnp.sum(swap(sums, "core").astype(F32), axis=0)

    def joined(array, width):
        first, second = array[: 8 * width], array[8 * width :]
        first = first.reshape((8, width) + array.shape[1:])
        second = jnp.broadcast_to(second[None], (8,) + second.shape)
        return jnp.concatenate([first, second], axis=1).astype(BF16)

    sums = jnp.sum(swap(joined(sums, 8), YX).astype(F32), axis=0)
    sums = jnp.sum(swap(joined(sums, 1), "z").astype(F32), axis=0)
    sums = jnp.sum(spread(sums.astype(BF16), "yh", 4).astype(F32), axis=0)
    sums = spread(sums, "core", 2)
    grad_out_proj = sums[:, 0].transpose(2, 0, 1, 3).reshape(8, model)
    grad_kernel = sums[:, 1:].transpose(1, 3, 0, 2, 4).reshape(32, model)[:KW]
    return layer_out[None], grad_mid[None], grad_out_proj, grad_kernel


def solution(mesh):
    split = Mesh(mesh.devices.reshape(4, 2, 2, 4, 8), ("yh", "core", "yl", "x", "z"))
    rows = P(("yh", "core"), SEQ, None)
    return jax.shard_map(
        body,
        mesh=split,
        in_specs=(rows, rows, rows, rows, P(), P(None, SEQ), P(), P(), P(), rows),
        out_specs=(rows, rows, P(SEQ, None), P()),
        check_vma=False,
    )
```

```python
import math

import jax
import jax.numpy as jnp
from jax import lax
from jax.experimental import pallas as pl
from jax.experimental.pallas import tpu as pltpu
from jax.sharding import Mesh, PartitionSpec as P


HEADS = 8
DH = 64
KW = 31
norm_epsilon = 1e-05

F32 = jnp.float32
BF16 = jnp.bfloat16

YX = ("yl", "xh", "xl")
NEAR = ("yl", "xl")
SEQ = ("yl", "xh", "xl", "z")
NT = (((1,), (1,)), ((), ()))


def pack_kernel(q_ref, k_ref, v_ref, w_ref, o_ref):
    for pair in range(HEADS // 2):
        cols = pl.ds(pair * 128, 128)
        q_t = q_ref[:, cols].astype(F32).T.astype(BF16)
        v_t = v_ref[:, cols].astype(F32).T.astype(BF16)
        upper = k_ref[0:64, cols].astype(F32)
        lower = k_ref[64:128, cols].astype(F32)
        lane = lax.broadcasted_iota(jnp.int32, upper.shape, 1)
        first = jnp.where(lane < 64, upper, pltpu.roll(lower, 64, 1)).astype(BF16)
        second = jnp.where(lane < 64, pltpu.roll(upper, 64, 1), lower).astype(BF16)
        for half, packed in ((0, first), (1, second)):
            head = 2 * pair + half
            o_ref[head, 0] = q_t[half * 64 : half * 64 + 64]
            o_ref[head, 1] = packed
            o_ref[head, 2] = v_t[half * 64 : half * 64 + 64]
    for half in range(2):
        turned = jnp.concatenate(
            [
                w_ref[half * 256 + b * 128 : half * 256 + b * 128 + 128, :].astype(F32).T
                for b in range(2)
            ],
            axis=0,
        ).astype(BF16)
        for head in range(HEADS):
            o_ref[head, 3 + half] = turned


def pack(q, k, v, w):
    return pl.pallas_call(
        pack_kernel,
        out_shape=jax.ShapeDtypeStruct((HEADS, 5, 64, 128), BF16),
    )(q, k, v, w)


SCALE = DH ** (-0.5) * math.log2(math.e)
QB = 256
SMALLEST = 2.0**-90
COST = pl.CostEstimate(flops=2**34, transcendentals=2**23, bytes_accessed=2**21)


def block_of(kv_ref, start, sources):
    packed = kv_ref[pl.ds(start, sources), 0].reshape(sources * 64, 128)
    keys = jnp.concatenate([packed, packed], axis=1)
    values = jnp.concatenate([kv_ref[start + s, 1] for s in range(sources)], axis=1)
    return keys, jnp.concatenate([values, jnp.ones((16, sources * 128), BF16)], axis=0)


def interleave(p_lo, p_hi, sources):
    pieces = []
    for s in range(sources):
        pieces.append(p_lo[s * 64 : s * 64 + 64])
        pieces.append(p_hi[s * 64 : s * 64 + 64])
    return jnp.concatenate(pieces, axis=0)


def attend_kernel(q_ref, kv_ref, o_ref, r_lo, r_hi, top, acc):
    count = q_ref.shape[0]
    sources = kv_ref.shape[0]
    blocks = count * 128 // QB
    group = 16
    whole = sources

    lane = lax.broadcasted_iota(jnp.int32, (128, 128), 1) < 64
    row = lax.broadcasted_iota(jnp.int32, (128, 128), 0) < 64
    same = (lane == row).astype(BF16)

    def longest(i, so_far):
        wide = kv_ref[pl.ds(i * group, group), 0].reshape(group * 64, 128).astype(F32)
        squares = (wide * wide).astype(BF16)
        return jnp.maximum(
            so_far,
            jnp.max(jnp.dot(squares, same, preferred_element_type=F32), axis=0, keepdims=True),
        )

    key_square = jnp.max(
        lax.fori_loop(0, sources // group, longest, jnp.zeros((1, 128), F32)),
        axis=1,
        keepdims=True,
    ) * 1.02

    for i in range(count):
        scaled = q_ref[i].astype(F32) * SCALE
        high = scaled.astype(BF16)
        low = (scaled - high.astype(F32)).astype(BF16)
        none = jnp.zeros_like(high)
        cols = pl.ds(i * 128, 128)
        r_lo[:, cols] = jnp.concatenate([high, none, low, none], axis=0)
        r_hi[:, cols] = jnp.concatenate([none, high, none, low], axis=0)
        top[:, cols] = jnp.sqrt(jnp.sum(scaled * scaled, axis=0, keepdims=True) * key_square)
    acc[...] = jnp.zeros(acc.shape, F32)

    def direct(i, carry):
        keys, values = block_of(kv_ref, i * whole, whole)
        for block in range(blocks):
            cols = pl.ds(block * QB, QB)
            bound = top[:, cols]
            s_lo = jnp.dot(keys, r_lo[:, cols], preferred_element_type=F32)
            p_lo = jnp.exp2(s_lo - bound).astype(BF16)
            s_hi = jnp.dot(keys, r_hi[:, cols], preferred_element_type=F32)
            p_hi = jnp.exp2(s_hi - bound).astype(BF16)
            acc[:, cols] += jnp.dot(
                values, interleave(p_lo, p_hi, whole), preferred_element_type=F32
            )
        return carry

    lax.fori_loop(0, sources // whole, direct, 0)

    @pl.when(jnp.min(acc[64:65]) < SMALLEST)
    def _():
        top[...] = jnp.full(top.shape, -jnp.inf, F32)
        acc[...] = jnp.zeros(acc.shape, F32)

        def online(i, carry):
            keys, values = block_of(kv_ref, i, 1)
            for block in range(blocks):
                cols = pl.ds(block * QB, QB)
                s_lo = jnp.dot(keys, r_lo[:, cols], preferred_element_type=F32)
                s_hi = jnp.dot(keys, r_hi[:, cols], preferred_element_type=F32)
                before = top[:, cols]
                highest = jnp.maximum(
                    before, jnp.max(jnp.maximum(s_lo, s_hi), axis=0, keepdims=True)
                )
                top[:, cols] = highest
                p_lo = jnp.exp2(s_lo - highest).astype(BF16)
                p_hi = jnp.exp2(s_hi - highest).astype(BF16)
                mixed = jnp.dot(values, interleave(p_lo, p_hi, 1), preferred_element_type=F32)
                acc[:, cols] = acc[:, cols] * jnp.exp2(before - highest) + mixed
            return carry

        lax.fori_loop(0, sources, online, 0)

    done = (acc[0:64] / acc[64:65]).astype(BF16)
    level = top[...] + jnp.log2(acc[64:65])
    high = level.astype(BF16)
    rest = level - high.astype(F32)
    middle = rest.astype(BF16)
    low = (rest - middle.astype(F32)).astype(BF16)
    for i in range(count):
        cols = slice(i * 128, i * 128 + 128)
        o_ref[i, 0:64] = done[:, cols]
        row = lax.broadcasted_iota(jnp.int32, (16, 128), 0)
        o_ref[i, 64:80] = jnp.where(
            row == 0,
            high[:, cols].astype(F32),
            jnp.where(row == 1, middle[:, cols].astype(F32), low[:, cols].astype(F32)),
        ).astype(BF16)


def attend(q_t, kv):
    count = q_t.shape[0]
    return pl.pallas_call(
        attend_kernel,
        out_shape=jax.ShapeDtypeStruct((count, 80, 128), BF16),
        scratch_shapes=[
            pltpu.VMEM((256, count * 128), BF16),
            pltpu.VMEM((256, count * 128), BF16),
            pltpu.VMEM((1, count * 128), F32),
            pltpu.VMEM((80, count * 128), F32),
        ],
        cost_estimate=COST,
        compiler_params=pltpu.CompilerParams(vmem_limit_bytes=56 * 1024 * 1024),
    )(q_t, kv)


STEPS = 4


def columns_of(w_ref, half):
    count = w_ref.shape[1] * 32
    return jnp.concatenate(
        [w_ref[half, :, b].reshape(count, 128) for b in range(4)], axis=1
    )


def gate_kernel(
    core_ref, att_ref, out_proj_ref, residual_ref, gain_ref, cot_ref, own_ref, other_ref,
    mid_ref, hat_ref, rscale_ref, value_ref, gate_ref, gated_ref, first_ref, last_ref, joined_ref,
    normed,
):
    step = pl.program_id(0)
    core = core_ref[0]
    half = normed.shape[2]

    @pl.when(step == 0)
    def _():
        heads = []
        for head in range(att_ref.shape[1]):
            parts = [att_ref[side, head].astype(F32) for side in range(2)]
            levels = [part[64:65] + part[65:66] + part[66:67] for part in parts]
            highest = jnp.maximum(levels[0], levels[1])
            shares = [jnp.exp2(level - highest) for level in levels]
            heads.append(
                (parts[0][0:64] * shares[0] + parts[1][0:64] * shares[1])
                / (shares[0] + shares[1])
            )
        joined = jnp.concatenate(heads, axis=0)
        joined_ref[...] = joined.astype(BF16)
        att = joined.T.astype(BF16)
        mid = (
            residual_ref[...].astype(F32)
            + jnp.dot(att, out_proj_ref[...], preferred_element_type=F32)
        ).astype(BF16)
        mid_ref[...] = mid
        wide = mid.astype(F32)
        centered = wide - jnp.mean(wide, axis=1, keepdims=True)
        rscale = lax.rsqrt(jnp.mean(centered * centered, axis=1, keepdims=True) + norm_epsilon)
        hat = centered * rscale
        hat_ref[...] = hat
        rscale_ref[...] = jnp.broadcast_to(rscale, rscale_ref.shape)
        scaled = (hat * gain_ref[...]).astype(BF16)
        normed[0] = scaled[:, :half]
        normed[1] = scaled[:, half:]

    def project(part):
        return lax.dot_general(
            normed[core], columns_of(own_ref, part), NT, preferred_element_type=F32
        ) + lax.dot_general(
            normed[1 - core], columns_of(other_ref, part), NT, preferred_element_type=F32
        )

    value = project(0)
    gate = jax.nn.sigmoid(project(1))
    value_ref[...] = value
    gate_ref[...] = gate
    gated = (value * gate).astype(BF16)
    gated_ref[...] = gated
    rows = gated.shape[0]
    first_ref[0:32] = gated[0:32]
    first_ref[32:48] = cot_ref[0:16]
    last_ref[0:32] = gated[rows - 32 :]
    last_ref[32:48] = cot_ref[rows - 16 :]


def gate(core, att, out_proj, residual, gain, cot, own, other):
    rows, model = residual.shape
    part = model // STEPS
    whole = lambda *shape: pl.BlockSpec(shape, lambda i: (0,) * len(shape))
    block = lambda count: pl.BlockSpec((count, part), lambda i: (0, i))
    weights = pl.BlockSpec((2, part // 32, 4, 32, 128), lambda i: (0, i, 0, 0, 0))
    array = jax.ShapeDtypeStruct
    return pl.pallas_call(
        gate_kernel,
        grid=(STEPS,),
        in_specs=[
            pl.BlockSpec(memory_space=pltpu.SMEM),
            whole(*att.shape),
            whole(*out_proj.shape),
            whole(rows, model),
            whole(1, model),
            block(rows),
            weights,
            weights,
        ],
        out_specs=[
            whole(rows, model),
            whole(rows, model),
            whole(rows, 128),
            block(rows),
            block(rows),
            block(rows),
            block(48),
            block(48),
            whole(HEADS * DH, rows),
        ],
        out_shape=[
            array((rows, model), BF16),
            array((rows, model), F32),
            array((rows, 128), F32),
            array((rows, model), F32),
            array((rows, model), F32),
            array((rows, model), BF16),
            array((48, model), BF16),
            array((48, model), BF16),
            array((HEADS * DH, rows), BF16),
        ],
        scratch_shapes=[pltpu.VMEM((2, rows, model // 2), BF16)],
        compiler_params=pltpu.CompilerParams(vmem_limit_bytes=56 * 1024 * 1024),
    )(core, att, out_proj, residual, gain, cot, own, other)


def back_kernel(
    core_ref, before_ref, after_ref, gated_ref, cot_before_ref, cot_after_ref, cot_ref,
    conv_out_ref, taps_ref, value_ref, gate_ref, own_ref, other_ref, mid_ref, hat_ref, rscale_ref,
    gain_ref, att_ref,
    layer_ref, grad_mid_ref, sums_ref,
    cot_wide, padded, gradient, layer_sum, normed_grad,
):
    step = pl.program_id(0)
    core = core_ref[0]
    rows = gated_ref.shape[0]
    tiles = padded.shape[0]

    @pl.when(step == 0)
    def _():
        cot_wide[0:16] = cot_before_ref[32:48]
        cot_wide[16 : 16 + rows] = cot_ref[...]
        cot_wide[16 + rows : 32 + rows] = cot_after_ref[32:48]
        layer_sum[...] = jnp.zeros(layer_sum.shape, F32)
        normed_grad[...] = jnp.zeros(normed_grad.shape, F32)

    for t in range(tiles):
        lanes = slice(t * 128, t * 128 + 128)
        padded[t, 0:32] = before_ref[0:32, lanes].astype(F32)
        padded[t, 32 : 32 + rows] = gated_ref[:, lanes].astype(F32)
        padded[t, 32 + rows : 64 + rows] = after_ref[0:32, lanes].astype(F32)

    weights = conv_out_ref[...]
    grad_act = lax.dot_general(cot_wide[...], weights, NT, preferred_element_type=F32)
    acts = []
    chunk = (rows + 32) // 2
    for t in range(tiles):
        lanes = slice(t * 128, t * 128 + 128)
        pieces = []
        for part in range(2):
            begin = part * chunk
            conv = jnp.zeros((chunk, 128), F32)
            for k in range(KW):
                conv = conv + taps_ref[k : k + 1, lanes] * padded[t, pl.ds(begin + k + 1, chunk)]
            sig = jax.nn.sigmoid(conv)
            pieces.append(conv * sig)
            gradient[t, begin : begin + chunk] = (
                (grad_act[begin : begin + chunk, lanes] * sig * (1.0 + conv * (1.0 - sig)))
                .astype(BF16)
                .astype(F32)
            )
        acts.append(jnp.concatenate(pieces, axis=0)[16 : 16 + rows])
    act = jnp.concatenate(acts, axis=1).astype(BF16)
    layer_sum[...] += jnp.dot(act, weights, preferred_element_type=F32)

    gated_grads = []
    for t in range(tiles):
        lanes = slice(t * 128, t * 128 + 128)
        pieces = []
        for part in range(2):
            begin = part * (rows // 2)
            total = jnp.zeros((rows // 2, 128), F32)
            for k in range(KW):
                total = total + taps_ref[k : k + 1, lanes] * gradient[
                    t, pl.ds(begin + 31 - k, rows // 2)
                ]
            pieces.append(total)
        gated_grads.append(jnp.concatenate(pieces, axis=0))

        inner = gradient[t, 16 : 16 + rows]
        terms = []
        for k in range(KW):
            terms.append(
                jnp.sum(padded[t, pl.ds(k + 17, rows)] * inner, axis=0, keepdims=True)
            )
        terms.append(jnp.zeros((1, 128), F32))
        tile = step * tiles + t
        sums_ref[tile // 4, 64:68, tile % 4] = (
            jnp.concatenate(terms, axis=0).astype(BF16).reshape(4, 8, 128)
        )

    grad_gated = jnp.concatenate(gated_grads, axis=1)
    value = value_ref[...]
    gate = gate_ref[...]
    to_value = (grad_gated * gate).astype(BF16)
    to_gate = (grad_gated * value * gate * (1.0 - gate)).astype(BF16)
    for place, ref in ((core, own_ref), (1 - core, other_ref)):
        normed_grad[place] += jnp.dot(
            to_value, columns_of(ref, 0), preferred_element_type=F32
        ) + jnp.dot(to_gate, columns_of(ref, 1), preferred_element_type=F32)

    @pl.when(step == pl.num_programs(0) - 1)
    def _():
        layer_ref[...] = (mid_ref[...].astype(F32) + layer_sum[...]).astype(BF16)
        hat = hat_ref[...]
        scaled = jnp.concatenate([normed_grad[0], normed_grad[1]], axis=1) * gain_ref[...]
        inner = (
            scaled
            - jnp.mean(scaled, axis=1, keepdims=True)
            - hat * jnp.mean(scaled * hat, axis=1, keepdims=True)
        )
        grad_mid = (cot_ref_f32(cot_ref) + rscale_ref[:, 0:1] * inner).astype(BF16)
        grad_mid_ref[...] = grad_mid
        for c in range(2):
            for b in range(4):
                cols = slice(c * 512 + b * 128, c * 512 + b * 128 + 128)
                product = jnp.dot(att_ref[...], grad_mid[:, cols], preferred_element_type=F32)
                sums_ref[c, 0:64, b] = product.astype(BF16).reshape(64, 8, 128)


def cot_ref_f32(ref):
    return ref[...].astype(F32)


def back(core, before, after, gated, cot, conv_out, taps, value, gate_half, own, other, mid, hat,
         rscale, gain, att):
    rows, model = gated.shape
    part = model // STEPS
    whole = lambda *shape: pl.BlockSpec(shape, lambda i: (0,) * len(shape))
    block = lambda count: pl.BlockSpec((count, part), lambda i: (0, i))
    weights = pl.BlockSpec((2, part // 32, 4, 32, 128), lambda i: (0, i, 0, 0, 0))
    array = jax.ShapeDtypeStruct
    return pl.pallas_call(
        back_kernel,
        grid=(STEPS,),
        in_specs=[
            pl.BlockSpec(memory_space=pltpu.SMEM),
            block(48),
            block(48),
            block(rows),
            whole(48, model),
            whole(48, model),
            whole(rows, model),
            pl.BlockSpec((part, model), lambda i: (i, 0)),
            block(KW + 1),
            block(rows),
            block(rows),
            weights,
            weights,
            whole(rows, model),
            whole(rows, model),
            whole(rows, 128),
            whole(1, model),
            whole(*att.shape),
        ],
        out_specs=[
            whole(rows, model),
            whole(rows, model),
            whole(2, 68, 4, 8, 128),
        ],
        out_shape=[
            array((rows, model), BF16),
            array((rows, model), BF16),
            array((2, 68, 4, 8, 128), BF16),
        ],
        scratch_shapes=[
            pltpu.VMEM((rows + 32, model), BF16),
            pltpu.VMEM((part // 128, rows + 64, 128), F32),
            pltpu.VMEM((part // 128, rows + 32, 128), F32),
            pltpu.VMEM((rows, model), F32),
            pltpu.VMEM((2, rows, model // 2), F32),
        ],
        compiler_params=pltpu.CompilerParams(vmem_limit_bytes=56 * 1024 * 1024),
    )(core, before, after, gated, before, after, cot, conv_out, taps, value, gate_half, own, other,
      mid, hat, rscale, gain, att)


def swap(array, axes):
    return lax.all_to_all(array, axes, split_axis=0, concat_axis=0, tiled=True)


def spread(array, axes, count):
    return swap(jnp.broadcast_to(array[None], (count,) + array.shape), axes)


def body(
    queries, keys, values, residual, out_proj, conv_in, conv_out, depth_kernel, norm_gain, cotangent
):
    model = residual.shape[2]
    core = lax.axis_index("core")
    place = core.astype(jnp.int32).reshape(1)
    gain = norm_gain.reshape(1, model)
    cot = cotangent[0]
    taps = jnp.pad(depth_kernel.astype(F32), ((0, 1), (0, 0)))

    share = lax.dynamic_slice_in_dim(conv_in, core * (model // 2), model // 2, axis=0)
    sent = pack(queries[0], keys[0], values[0], share)
    got = swap(sent, "z")
    mine = got[:, 0]
    theirs = lax.ppermute(mine, "xh", [(0, 1), (1, 0)])
    kv = spread(got[:, 1:3], NEAR, 4).reshape(32, 2, 64, 128)
    upper = lax.axis_index("xh") == 1
    query_blocks = jnp.concatenate(
        [jnp.where(upper, theirs, mine), jnp.where(upper, mine, theirs)], axis=0
    )
    own = spread(got[:, 3:5], YX, 8).reshape(2, 32, 4, 32, 128)
    attended = attend(query_blocks, kv)
    other = lax.ppermute(own, "core", [(0, 1), (1, 0)])
    parts = swap(attended, ("xh", "z")).reshape(2, HEADS, 80, 128)

    mid, hat, rscale, value_half, gate_half, gated, first, last, att = gate(
        place, parts, out_proj, residual[0], gain, cot, own, other
    )
    count = 64
    before = lax.ppermute(last, SEQ, [(i, i + 1) for i in range(count - 1)])
    after = lax.ppermute(first, SEQ, [(i + 1, i) for i in range(count - 1)])
    layer_out, grad_mid, sums = back(
        place, before, after, gated, cot, conv_out, taps, value_half, gate_half, own, other, mid,
        hat, rscale, gain, att,
    )

    sums = jnp.sum(swap(sums, "core").astype(F32), axis=0)

    def joined(array, width):
        first, second = array[: 8 * width], array[8 * width :]
        first = first.reshape((8, width) + array.shape[1:])
        second = jnp.broadcast_to(second[None], (8,) + second.shape)
        return jnp.concatenate([first, second], axis=1).astype(BF16)

    sums = jnp.sum(swap(joined(sums, 8), YX).astype(F32), axis=0)
    sums = jnp.sum(swap(joined(sums, 1), "z").astype(F32), axis=0)
    sums = jnp.sum(spread(sums.astype(BF16), "yh", 4).astype(F32), axis=0)
    sums = spread(sums, "core", 2)
    grad_out_proj = sums[:, 0].transpose(2, 0, 1, 3).reshape(8, model)
    grad_kernel = sums[:, 1:].transpose(1, 3, 0, 2, 4).reshape(32, model)[:KW]
    return layer_out[None], grad_mid[None], grad_out_proj, grad_kernel


def solution(mesh):
    split = Mesh(mesh.devices.reshape(4, 2, 2, 2, 2, 8), ("yh", "core", "yl", "xh", "xl", "z"))
    rows = P(("yh", "core"), SEQ, None)
    return jax.shard_map(
        body,
        mesh=split,
        in_specs=(rows, rows, rows, rows, P(), P(None, SEQ), P(), P(), P(), rows),
        out_specs=(rows, rows, P(SEQ, None), P()),
        check_vma=False,
    )
```

```python
import math

import jax
import jax.numpy as jnp
from jax import lax
from jax.experimental import pallas as pl
from jax.experimental.pallas import tpu as pltpu
from jax.sharding import Mesh, PartitionSpec as P


HEADS = 8
DH = 64
KW = 31
norm_epsilon = 1e-05

F32 = jnp.float32
BF16 = jnp.bfloat16

YX = ("yl", "xh", "xl")
NEAR = ("yl", "xl")
SEQ = ("yl", "xh", "xl", "z")
NT = (((1,), (1,)), ((), ()))


def pack_kernel(core_ref, q_ref, k_ref, v_ref, w_ref, o_ref):
    for pair in range(HEADS // 2):
        cols = pl.ds(pair * 128, 128)
        q_t = q_ref[:, cols].astype(F32).T.astype(BF16)
        v_t = v_ref[:, cols].astype(F32).T.astype(BF16)
        upper = k_ref[0:64, cols].astype(F32)
        lower = k_ref[64:128, cols].astype(F32)
        lane = lax.broadcasted_iota(jnp.int32, upper.shape, 1)
        first = jnp.where(lane < 64, upper, pltpu.roll(lower, 64, 1)).astype(BF16)
        second = jnp.where(lane < 64, pltpu.roll(upper, 64, 1), lower).astype(BF16)
        for half, packed in ((0, first), (1, second)):
            head = 2 * pair + half
            o_ref[head, 0] = q_t[half * 64 : half * 64 + 64]
            o_ref[head, 1] = packed
            o_ref[head, 2] = v_t[half * 64 : half * 64 + 64]
    features = w_ref.shape[1] // 2
    share = jnp.where(
        core_ref[0] == 0, w_ref[:, :features].astype(F32), w_ref[:, features:].astype(F32)
    ).astype(BF16)
    for half in range(2):
        blocks = [share[:, (2 * half + b) * 128 : (2 * half + b + 1) * 128] for b in range(2)]
        for head in range(HEADS):
            o_ref[head, 3 + half] = jnp.concatenate(blocks, axis=0)


def pack(core, q, k, v, w):
    local = pl.BlockSpec(memory_space=pltpu.VMEM)
    return pl.pallas_call(
        pack_kernel,
        in_specs=[pl.BlockSpec(memory_space=pltpu.SMEM), local, local, local, local],
        out_shape=jax.ShapeDtypeStruct((HEADS, 5, 64, 128), BF16),
        compiler_params=pltpu.CompilerParams(vmem_limit_bytes=56 * 1024 * 1024),
    )(core, q, k, v, w)


SCALE = DH ** (-0.5) * math.log2(math.e)
QB = 256
SMALLEST = 2.0**-90
COST = pl.CostEstimate(flops=2**34, transcendentals=2**23, bytes_accessed=2**21)


def block_of(kv_ref, start, sources):
    packed = kv_ref[pl.ds(start, sources), 0].reshape(sources * 64, 128)
    keys = jnp.concatenate([packed, packed], axis=1)
    values = jnp.concatenate([kv_ref[start + s, 1] for s in range(sources)], axis=1)
    return keys, jnp.concatenate([values, jnp.ones((16, sources * 128), BF16)], axis=0)


def interleave(p_lo, p_hi, sources):
    pieces = []
    for s in range(sources):
        pieces.append(p_lo[s * 64 : s * 64 + 64])
        pieces.append(p_hi[s * 64 : s * 64 + 64])
    return jnp.concatenate(pieces, axis=0)


def attend_kernel(q_ref, kv_ref, o_ref, r_lo, r_hi, top, acc):
    count = q_ref.shape[0]
    sources = kv_ref.shape[0]
    blocks = count * 128 // QB
    group = 16
    whole = sources

    lane = lax.broadcasted_iota(jnp.int32, (128, 128), 1) < 64
    row = lax.broadcasted_iota(jnp.int32, (128, 128), 0) < 64
    same = (lane == row).astype(BF16)

    def longest(i, so_far):
        wide = kv_ref[pl.ds(i * group, group), 0].reshape(group * 64, 128).astype(F32)
        squares = (wide * wide).astype(BF16)
        return jnp.maximum(
            so_far,
            jnp.max(jnp.dot(squares, same, preferred_element_type=F32), axis=0, keepdims=True),
        )

    key_square = jnp.max(
        lax.fori_loop(0, sources // group, longest, jnp.zeros((1, 128), F32)),
        axis=1,
        keepdims=True,
    ) * 1.02

    for i in range(count):
        scaled = q_ref[i].astype(F32) * SCALE
        high = scaled.astype(BF16)
        low = (scaled - high.astype(F32)).astype(BF16)
        none = jnp.zeros_like(high)
        cols = pl.ds(i * 128, 128)
        r_lo[:, cols] = jnp.concatenate([high, none, low, none], axis=0)
        r_hi[:, cols] = jnp.concatenate([none, high, none, low], axis=0)
        top[:, cols] = jnp.sqrt(jnp.sum(scaled * scaled, axis=0, keepdims=True) * key_square)
    acc[...] = jnp.zeros(acc.shape, F32)

    def direct(i, carry):
        keys, values = block_of(kv_ref, i * whole, whole)
        for block in range(blocks):
            cols = pl.ds(block * QB, QB)
            bound = top[:, cols]
            s_lo = jnp.dot(keys, r_lo[:, cols], preferred_element_type=F32)
            p_lo = jnp.exp2(s_lo - bound).astype(BF16)
            s_hi = jnp.dot(keys, r_hi[:, cols], preferred_element_type=F32)
            p_hi = jnp.exp2(s_hi - bound).astype(BF16)
            acc[:, cols] += jnp.dot(
                values, interleave(p_lo, p_hi, whole), preferred_element_type=F32
            )
        return carry

    lax.fori_loop(0, sources // whole, direct, 0)

    @pl.when(jnp.min(acc[64:65]) < SMALLEST)
    def _():
        top[...] = jnp.full(top.shape, -jnp.inf, F32)
        acc[...] = jnp.zeros(acc.shape, F32)

        def online(i, carry):
            keys, values = block_of(kv_ref, i, 1)
            for block in range(blocks):
                cols = pl.ds(block * QB, QB)
                s_lo = jnp.dot(keys, r_lo[:, cols], preferred_element_type=F32)
                s_hi = jnp.dot(keys, r_hi[:, cols], preferred_element_type=F32)
                before = top[:, cols]
                highest = jnp.maximum(
                    before, jnp.max(jnp.maximum(s_lo, s_hi), axis=0, keepdims=True)
                )
                top[:, cols] = highest
                p_lo = jnp.exp2(s_lo - highest).astype(BF16)
                p_hi = jnp.exp2(s_hi - highest).astype(BF16)
                mixed = jnp.dot(values, interleave(p_lo, p_hi, 1), preferred_element_type=F32)
                acc[:, cols] = acc[:, cols] * jnp.exp2(before - highest) + mixed
            return carry

        lax.fori_loop(0, sources, online, 0)

    done = (acc[0:64] / acc[64:65]).astype(BF16)
    level = top[...] + jnp.log2(acc[64:65])
    high = level.astype(BF16)
    rest = level - high.astype(F32)
    middle = rest.astype(BF16)
    low = (rest - middle.astype(F32)).astype(BF16)
    for i in range(count):
        cols = slice(i * 128, i * 128 + 128)
        o_ref[i, 0:64] = done[:, cols]
        row = lax.broadcasted_iota(jnp.int32, (16, 128), 0)
        o_ref[i, 64:80] = jnp.where(
            row == 0,
            high[:, cols].astype(F32),
            jnp.where(row == 1, middle[:, cols].astype(F32), low[:, cols].astype(F32)),
        ).astype(BF16)


def attend(q_t, kv):
    count = q_t.shape[0]
    return pl.pallas_call(
        attend_kernel,
        out_shape=jax.ShapeDtypeStruct((count, 80, 128), BF16),
        scratch_shapes=[
            pltpu.VMEM((256, count * 128), BF16),
            pltpu.VMEM((256, count * 128), BF16),
            pltpu.VMEM((1, count * 128), F32),
            pltpu.VMEM((80, count * 128), F32),
        ],
        cost_estimate=COST,
        compiler_params=pltpu.CompilerParams(vmem_limit_bytes=24 * 1024 * 1024),
    )(q_t, kv)


STEPS = 4


def columns_of(w_ref, half):
    count = w_ref.shape[1] * 32
    return jnp.concatenate(
        [w_ref[half, :, b].reshape(count, 128) for b in range(4)], axis=1
    )


def gate_kernel(
    core_ref, att_ref, out_proj_ref, residual_ref, gain_ref, cot_ref, own_ref, other_ref,
    mid_ref, hat_ref, rscale_ref, value_ref, gate_ref, gated_ref, first_ref, last_ref, joined_ref,
    normed,
):
    step = pl.program_id(0)
    core = core_ref[0]
    half = normed.shape[2]

    @pl.when(step == 0)
    def _():
        heads = []
        for head in range(att_ref.shape[1]):
            parts = [att_ref[side, head].astype(F32) for side in range(2)]
            levels = [part[64:65] + part[65:66] + part[66:67] for part in parts]
            highest = jnp.maximum(levels[0], levels[1])
            shares = [jnp.exp2(level - highest) for level in levels]
            heads.append(
                (parts[0][0:64] * shares[0] + parts[1][0:64] * shares[1])
                / (shares[0] + shares[1])
            )
        joined = jnp.concatenate(heads, axis=0)
        joined_ref[...] = joined.astype(BF16)
        att = joined.T.astype(BF16)
        mid = (
            residual_ref[...].astype(F32)
            + jnp.dot(att, out_proj_ref[...], preferred_element_type=F32)
        ).astype(BF16)
        mid_ref[...] = mid
        wide = mid.astype(F32)
        centered = wide - jnp.mean(wide, axis=1, keepdims=True)
        rscale = lax.rsqrt(jnp.mean(centered * centered, axis=1, keepdims=True) + norm_epsilon)
        hat = centered * rscale
        hat_ref[...] = hat
        rscale_ref[...] = jnp.broadcast_to(rscale, rscale_ref.shape)
        scaled = (hat * gain_ref[...]).astype(BF16)
        normed[0] = scaled[:, :half]
        normed[1] = scaled[:, half:]

    def project(part):
        return lax.dot_general(
            normed[core], columns_of(own_ref, part), NT, preferred_element_type=F32
        ) + lax.dot_general(
            normed[1 - core], columns_of(other_ref, part), NT, preferred_element_type=F32
        )

    value = project(0)
    gate = jax.nn.sigmoid(project(1))
    value_ref[...] = value
    gate_ref[...] = gate
    gated = (value * gate).astype(BF16)
    gated_ref[...] = gated
    rows = gated.shape[0]
    first_ref[0:32] = gated[0:32]
    first_ref[32:48] = cot_ref[0:16]
    last_ref[0:32] = gated[rows - 32 :]
    last_ref[32:48] = cot_ref[rows - 16 :]


def gate(core, att, out_proj, residual, gain, cot, own, other):
    rows, model = residual.shape
    part = model // STEPS
    whole = lambda *shape: pl.BlockSpec(shape, lambda i: (0,) * len(shape))
    block = lambda count: pl.BlockSpec((count, part), lambda i: (0, i))
    weights = pl.BlockSpec((2, part // 32, 4, 32, 128), lambda i: (0, i, 0, 0, 0))
    array = jax.ShapeDtypeStruct
    return pl.pallas_call(
        gate_kernel,
        grid=(STEPS,),
        in_specs=[
            pl.BlockSpec(memory_space=pltpu.SMEM),
            whole(*att.shape),
            whole(*out_proj.shape),
            whole(rows, model),
            whole(1, model),
            block(rows),
            weights,
            weights,
        ],
        out_specs=[
            whole(rows, model),
            whole(rows, model),
            whole(rows, 128),
            block(rows),
            block(rows),
            block(rows),
            block(48),
            block(48),
            whole(HEADS * DH, rows),
        ],
        out_shape=[
            array((rows, model), BF16),
            array((rows, model), F32),
            array((rows, 128), F32),
            array((rows, model), F32),
            array((rows, model), F32),
            array((rows, model), BF16),
            array((48, model), BF16),
            array((48, model), BF16),
            array((HEADS * DH, rows), BF16),
        ],
        scratch_shapes=[pltpu.VMEM((2, rows, model // 2), BF16)],
        compiler_params=pltpu.CompilerParams(vmem_limit_bytes=16 * 1024 * 1024),
    )(core, att, out_proj, residual, gain, cot, own, other)


def back_kernel(
    core_ref, before_ref, after_ref, gated_ref, cot_before_ref, cot_after_ref, cot_ref,
    conv_out_ref, taps_ref, value_ref, gate_ref, own_ref, other_ref, mid_ref, hat_ref, rscale_ref,
    gain_ref, att_ref,
    layer_ref, grad_mid_ref, sums_ref,
    cot_wide, padded, gradient, layer_sum, normed_grad,
):
    step = pl.program_id(0)
    core = core_ref[0]
    rows = gated_ref.shape[0]
    tiles = padded.shape[0]

    @pl.when(step == 0)
    def _():
        cot_wide[0:16] = cot_before_ref[32:48]
        cot_wide[16 : 16 + rows] = cot_ref[...]
        cot_wide[16 + rows : 32 + rows] = cot_after_ref[32:48]
        layer_sum[...] = jnp.zeros(layer_sum.shape, F32)
        normed_grad[...] = jnp.zeros(normed_grad.shape, F32)

    for t in range(tiles):
        lanes = slice(t * 128, t * 128 + 128)
        padded[t, 0:32] = before_ref[0:32, lanes].astype(F32)
        padded[t, 32 : 32 + rows] = gated_ref[:, lanes].astype(F32)
        padded[t, 32 + rows : 64 + rows] = after_ref[0:32, lanes].astype(F32)

    weights = conv_out_ref[...]
    grad_act = lax.dot_general(cot_wide[...], weights, NT, preferred_element_type=F32)
    acts = []
    chunk = (rows + 32) // 2
    for t in range(tiles):
        lanes = slice(t * 128, t * 128 + 128)
        pieces = []
        for part in range(2):
            begin = part * chunk
            conv = jnp.zeros((chunk, 128), F32)
            for k in range(KW):
                conv = conv + taps_ref[k : k + 1, lanes] * padded[t, pl.ds(begin + k + 1, chunk)]
            sig = jax.nn.sigmoid(conv)
            pieces.append(conv * sig)
            gradient[t, begin : begin + chunk] = (
                (grad_act[begin : begin + chunk, lanes] * sig * (1.0 + conv * (1.0 - sig)))
                .astype(BF16)
                .astype(F32)
            )
        acts.append(jnp.concatenate(pieces, axis=0)[16 : 16 + rows])
    act = jnp.concatenate(acts, axis=1).astype(BF16)
    layer_sum[...] += jnp.dot(act, weights, preferred_element_type=F32)

    gated_grads = []
    for t in range(tiles):
        lanes = slice(t * 128, t * 128 + 128)
        pieces = []
        for part in range(2):
            begin = part * (rows // 2)
            total = jnp.zeros((rows // 2, 128), F32)
            for k in range(KW):
                total = total + taps_ref[k : k + 1, lanes] * gradient[
                    t, pl.ds(begin + 31 - k, rows // 2)
                ]
            pieces.append(total)
        gated_grads.append(jnp.concatenate(pieces, axis=0))

        inner = gradient[t, 16 : 16 + rows]
        terms = []
        for k in range(KW):
            terms.append(
                jnp.sum(padded[t, pl.ds(k + 17, rows)] * inner, axis=0, keepdims=True)
            )
        terms.append(jnp.zeros((1, 128), F32))
        tile = step * tiles + t
        sums_ref[tile // 4, 64:68, tile % 4] = (
            jnp.concatenate(terms, axis=0).astype(BF16).reshape(4, 8, 128)
        )

    grad_gated = jnp.concatenate(gated_grads, axis=1)
    value = value_ref[...]
    gate = gate_ref[...]
    to_value = (grad_gated * gate).astype(BF16)
    to_gate = (grad_gated * value * gate * (1.0 - gate)).astype(BF16)
    for place, ref in ((core, own_ref), (1 - core, other_ref)):
        normed_grad[place] += jnp.dot(
            to_value, columns_of(ref, 0), preferred_element_type=F32
        ) + jnp.dot(to_gate, columns_of(ref, 1), preferred_element_type=F32)

    @pl.when(step == pl.num_programs(0) - 1)
    def _():
        layer_ref[...] = (mid_ref[...].astype(F32) + layer_sum[...]).astype(BF16)
        hat = hat_ref[...]
        scaled = jnp.concatenate([normed_grad[0], normed_grad[1]], axis=1) * gain_ref[...]
        inner = (
            scaled
            - jnp.mean(scaled, axis=1, keepdims=True)
            - hat * jnp.mean(scaled * hat, axis=1, keepdims=True)
        )
        grad_mid = (cot_ref_f32(cot_ref) + rscale_ref[:, 0:1] * inner).astype(BF16)
        grad_mid_ref[...] = grad_mid
        for c in range(2):
            for b in range(4):
                cols = slice(c * 512 + b * 128, c * 512 + b * 128 + 128)
                product = jnp.dot(att_ref[...], grad_mid[:, cols], preferred_element_type=F32)
                sums_ref[c, 0:64, b] = product.astype(BF16).reshape(64, 8, 128)


def cot_ref_f32(ref):
    return ref[...].astype(F32)


def back(core, before, after, gated, cot, conv_out, taps, value, gate_half, own, other, mid, hat,
         rscale, gain, att):
    rows, model = gated.shape
    part = model // STEPS
    whole = lambda *shape: pl.BlockSpec(shape, lambda i: (0,) * len(shape))
    block = lambda count: pl.BlockSpec((count, part), lambda i: (0, i))
    weights = pl.BlockSpec((2, part // 32, 4, 32, 128), lambda i: (0, i, 0, 0, 0))
    array = jax.ShapeDtypeStruct
    return pl.pallas_call(
        back_kernel,
        grid=(STEPS,),
        in_specs=[
            pl.BlockSpec(memory_space=pltpu.SMEM),
            block(48),
            block(48),
            block(rows),
            whole(48, model),
            whole(48, model),
            whole(rows, model),
            pl.BlockSpec((part, model), lambda i: (i, 0)),
            block(KW + 1),
            block(rows),
            block(rows),
            weights,
            weights,
            whole(rows, model),
            whole(rows, model),
            whole(rows, 128),
            whole(1, model),
            whole(*att.shape),
        ],
        out_specs=[
            whole(rows, model),
            whole(rows, model),
            whole(2, 68, 4, 8, 128),
        ],
        out_shape=[
            array((rows, model), BF16),
            array((rows, model), BF16),
            array((2, 68, 4, 8, 128), BF16),
        ],
        scratch_shapes=[
            pltpu.VMEM((rows + 32, model), BF16),
            pltpu.VMEM((part // 128, rows + 64, 128), F32),
            pltpu.VMEM((part // 128, rows + 32, 128), F32),
            pltpu.VMEM((rows, model), F32),
            pltpu.VMEM((2, rows, model // 2), F32),
        ],
        compiler_params=pltpu.CompilerParams(vmem_limit_bytes=20 * 1024 * 1024),
    )(core, before, after, gated, before, after, cot, conv_out, taps, value, gate_half, own, other,
      mid, hat, rscale, gain, att)


def swap(array, axes):
    return lax.all_to_all(array, axes, split_axis=0, concat_axis=0, tiled=True)


def spread(array, axes, count):
    return swap(jnp.broadcast_to(array[None], (count,) + array.shape), axes)


def body(
    queries, keys, values, residual, out_proj, conv_in, conv_out, depth_kernel, norm_gain, cotangent
):
    model = residual.shape[2]
    core = lax.axis_index("core")
    place = core.astype(jnp.int32).reshape(1)
    gain = norm_gain.reshape(1, model)
    cot = cotangent[0]
    taps = jnp.pad(depth_kernel.astype(F32), ((0, 1), (0, 0)))

    sent = pack(place, queries[0], keys[0], values[0], conv_in.T)
    got = swap(sent, "z")
    mine = got[:, 0]
    theirs = lax.ppermute(mine, "xh", [(0, 1), (1, 0)])
    kv = spread(got[:, 1:3], NEAR, 4).reshape(32, 2, 64, 128)
    upper = lax.axis_index("xh") == 1
    query_blocks = jnp.concatenate(
        [jnp.where(upper, theirs, mine), jnp.where(upper, mine, theirs)], axis=0
    )
    own = spread(got[:, 3:5], YX, 8).reshape(2, 32, 4, 32, 128)
    attended = attend(query_blocks, kv)
    other = lax.ppermute(own, "core", [(0, 1), (1, 0)])
    parts = swap(attended, ("xh", "z")).reshape(2, HEADS, 80, 128)

    mid, hat, rscale, value_half, gate_half, gated, first, last, att = gate(
        place, parts, out_proj, residual[0], gain, cot, own, other
    )
    count = 64
    before = lax.ppermute(last, SEQ, [(i, i + 1) for i in range(count - 1)])
    after = lax.ppermute(first, SEQ, [(i + 1, i) for i in range(count - 1)])
    layer_out, grad_mid, sums = back(
        place, before, after, gated, cot, conv_out, taps, value_half, gate_half, own, other, mid,
        hat, rscale, gain, att,
    )

    sums = jnp.sum(swap(sums, "core").astype(F32), axis=0)

    def joined(array, width):
        first, second = array[: 8 * width], array[8 * width :]
        first = first.reshape((8, width) + array.shape[1:])
        second = jnp.broadcast_to(second[None], (8,) + second.shape)
        return jnp.concatenate([first, second], axis=1).astype(BF16)

    sums = jnp.sum(swap(joined(sums, 8), YX).astype(F32), axis=0)
    sums = jnp.sum(swap(joined(sums, 1), "z").astype(F32), axis=0)
    sums = jnp.sum(spread(sums.astype(BF16), "yh", 4).astype(F32), axis=0)
    sums = spread(sums, "core", 2)
    grad_out_proj = sums[:, 0].transpose(2, 0, 1, 3).reshape(8, model)
    grad_kernel = sums[:, 1:].transpose(1, 3, 0, 2, 4).reshape(32, model)[:KW]
    return layer_out[None], grad_mid[None], grad_out_proj, grad_kernel


def solution(mesh):
    split = Mesh(mesh.devices.reshape(4, 2, 2, 2, 2, 8), ("yh", "core", "yl", "xh", "xl", "z"))
    rows = P(("yh", "core"), SEQ, None)
    return jax.shard_map(
        body,
        mesh=split,
        in_specs=(rows, rows, rows, rows, P(), P(None, SEQ), P(), P(), P(), rows),
        out_specs=(rows, rows, P(SEQ, None), P()),
        check_vma=False,
    )
```
